512 devices in a mesh: case: 8 (over x, core), elem: 64 (over y, z).
Axes of the slice: x: 4, y: 4, z: 16, core: 2. Of those that a mesh axis runs over, the one named last changes fastest.
Arguments:
- load_coef: bfloat16 [4096, 512], P(('case', 'elem')), may hold values from -13 to 13
- mantissa: bfloat16 [512, 3, 65536], P(None, None, 'elem'), may hold values from -0.25 to 0.25
- scale_exp: int32 [512, 3, 512], P(None, None, 'elem'), may hold values from -1 to 1
- lin_coef: float32 [2, 65536], P(None, 'elem'), may hold values from -0.5 to 0.5
- quad_coef: float32 [3, 65536], P(None, 'elem'), may hold values from 0.05 to 0.3
- cross_coef: float32 [65536], P('elem'), may hold values from -0.1 to 0.1
- ply_count: int32 [65536], P('elem'), may hold values from 0 to 7
- cotangent: float32 [4096], P('case'), may hold values from -6 to 6
Outputs:
- load_grad: float32 [4096, 512], P(('case', 'elem'))
- coef_grad: float32 [6, 65536], P(None, 'elem')
The draws below stay inside these ranges and needn't reach their ends.
All inputs are finite; a program needn't handle non-finite values.
Results may differ from the reference program's by a relative error of at most 0.0065.
Values may be sent and summed in bfloat16 or wider, within the bound.
A program may use at most 64 MiB of HBM per device.

```python
import math
import jax
import jax.numpy as jnp
import numpy as np
from jax import lax

U = 512
BLK = 128
CASES = 4096
COLS = 65536
N_ELEM = 64


def draw_load_coef(key, part):
    base = 0.5 * jax.random.normal(key, (CASES, U), jnp.float32)
    return jnp.clip(base, -3.0, 3.0).astype(jnp.bfloat16)


def plant(array, own_key, smallest, largest):
    shape = array.shape
    spot = [jax.random.randint(jax.random.fold_in(own_key, axis), (), 0, shape[axis]) for axis in range(len(shape))]
    array = array.at[tuple(spot)].set(smallest)
    longest = shape.index(max(shape))
    spot[longest] = (spot[longest] + 1) % shape[longest]
    return array.at[tuple(spot)].set(largest)


def steps_of(key, extent, cuts, smallest, high):
    gain = 1.0
    for axis_at, blocks in cuts:
        draws = jax.random.uniform(jax.random.fold_in(jax.random.fold_in(key, 6), axis_at), (blocks,), jnp.float32, smallest / len(cuts), high / len(cuts))
        gain = gain * jnp.repeat(jnp.exp(draws), extent[axis_at] // blocks).reshape((-1,) + (1,) * (len(extent) - 1 - axis_at))
    return gain


def rank_table(number_of, slope):
    weights = [(1 << 20) // math.isqrt(standing ** slope) + 1 for standing in range(1, number_of + 1)]
    deviation = 1 + sum(weights) // (1 << 30)
    return np.cumsum(np.array([max(1, weight // deviation) for weight in weights]))


def skewed_ids(key, dims, number_of, skew):
    grid = rank_table(number_of, skew)
    lot = jax.random.randint(jax.random.fold_in(key, 1), dims, 0, int(grid[number_of - 1]))
    standing = jnp.searchsorted(jnp.asarray(grid, jnp.int32), lot, side="right")
    return jax.random.permutation(jax.random.fold_in(key, 2), number_of)[standing].astype(jnp.int32)


def gaussian(rng, dims, deviation, bound, cuts=(), kind=jnp.bfloat16):
    result = deviation * jax.random.normal(rng, dims, jnp.float32)
    if cuts:
        result = result * steps_of(rng, dims, cuts, -0.22, 0.18)
    return jnp.clip(result, -bound, bound).astype(kind)


def setup_inputs(seed: int = 0) -> dict:
    seeds = jax.random.split(jax.random.key(seed), 9)
    return {
        "load_coef": draw_load_coef(jax.random.fold_in(seeds[8], 71), 0),
        "mantissa": gaussian(seeds[1], (U, 3, COLS), U ** -0.5, 0.25, ((2, 64),)),
        "scale_exp": plant(jax.random.randint(seeds[2], (U, 3, COLS // BLK), -1, 2), jax.random.fold_in(seeds[2], 1), -1, 1).astype(jnp.int32),
        "lin_coef": jnp.clip(jax.random.uniform(seeds[3], (2, COLS), jnp.float32, -0.5, 0.5) * steps_of(seeds[3], (2, COLS), ((1, 64),), -0.4, 0.0), -0.5, 0.5),
        "quad_coef": jnp.clip(jnp.exp(math.log(0.3) - 1.7917595 * jax.random.uniform(seeds[4], (3, COLS), jnp.float32) ** steps_of(seeds[4], (3, COLS), ((1, 64),), -0.2, 0.2)), 0.05, 0.3),
        "cross_coef": jnp.clip(jax.random.uniform(seeds[5], (COLS,), jnp.float32, -0.1, 0.1) * steps_of(seeds[5], (COLS,), ((0, 64),), -0.4, 0.0), -0.1, 0.1),
        "ply_count": plant(skewed_ids(seeds[6], (COLS,), 8, 2), jax.random.fold_in(seeds[6], 3), 0, 7).astype(jnp.int32),
        "cotangent": gaussian(seeds[7], (CASES,), 1.0, 6.0, ((0, 8),), jnp.float32),
    }


rho_value = 1.0


def dequant(mant, expo):
    units, comps, width = mant.shape
    blocks = expo.shape[-1]
    factor = jnp.exp2(expo.astype(jnp.float32)).astype(jnp.bfloat16)
    scaled = mant.reshape(units, comps, blocks, width // blocks) * factor[..., None]
    return scaled.reshape(units, comps * width)


def tsai_wu(first, second, shear, lin, quad, cross):
    return (lin[0] * first + lin[1] * second + quad[0] * first * first
            + quad[1] * second * second + quad[2] * shear * shear
            + 2.0 * cross * first * second)


def reference(load_coef, mantissa, scale_exp, lin_coef, quad_coef, cross_coef, ply_count, cotangent):
    nblk = N_ELEM
    width = mantissa.shape[2] // nblk
    mant_blocks = mantissa.reshape(U, 3, nblk, width).transpose(2, 0, 1, 3)
    exp_blocks = scale_exp.reshape(U, 3, nblk, -1).transpose(2, 0, 1, 3)
    lin_blocks = lin_coef.reshape(2, nblk, width).transpose(1, 0, 2)
    quad_blocks = quad_coef.reshape(3, nblk, width).transpose(1, 0, 2)
    cross_blocks = cross_coef.reshape(nblk, width)
    ply_blocks = (ply_count + 1).astype(jnp.float32).reshape(nblk, width)

    def forward(pieces):
        mant, expo = pieces
        fields = dequant(mant, expo)
        return jnp.dot(load_coef, fields, preferred_element_type=jnp.float32).reshape(-1, 3, width)

    stress = lax.map(forward, (mant_blocks, exp_blocks))
    index = tsai_wu(stress[:, :, 0], stress[:, :, 1], stress[:, :, 2],
                    lin_blocks.transpose(1, 0, 2)[:, :, None, :],
                    quad_blocks.transpose(1, 0, 2)[:, :, None, :],
                    cross_blocks[:, None, :])
    peak = jnp.max(index, axis=(0, 2))
    total = jnp.sum(ply_blocks[:, None, :] * jnp.exp(rho_value * (index - peak[None, :, None])), axis=(0, 2))
    envelope = peak + jnp.log(total) / rho_value

    def backward(carry, pieces):
        mant, expo, block_stress, block_index, lin, quad, cross, plies = pieces
        fields = dequant(mant, expo)
        first = block_stress[:, 0]
        second = block_stress[:, 1]
        shear = block_stress[:, 2]
        weight = cotangent[:, None] * plies[None, :] * jnp.exp(rho_value * (block_index - envelope[:, None]))
        grad_one = weight * (lin[0] + 2.0 * quad[0] * first + 2.0 * cross * second)
        grad_two = weight * (lin[1] + 2.0 * quad[1] * second + 2.0 * cross * first)
        grad_three = weight * (2.0 * quad[2] * shear)
        dstress = jnp.concatenate([grad_one, grad_two, grad_three], axis=1).astype(jnp.bfloat16)
        carry = carry + lax.dot_general(dstress, fields, (((1,), (1,)), ((), ())),
                                        preferred_element_type=jnp.float32)
        coefs = jnp.stack([jnp.sum(weight * first, axis=0), jnp.sum(weight * second, axis=0),
                           jnp.sum(weight * first * first, axis=0), jnp.sum(weight * second * second, axis=0),
                           jnp.sum(weight * shear * shear, axis=0), jnp.sum(weight * 2.0 * first * second, axis=0)])
        return carry, coefs

    start = jnp.zeros((load_coef.shape[0], U), jnp.float32)
    load_grad, coefs = lax.scan(backward, start, (mant_blocks, exp_blocks, stress, index,
                                                  lin_blocks, quad_blocks, cross_blocks, ply_blocks))
    coef_grad = coefs.transpose(1, 0, 2).reshape(6, -1)
    return load_grad, coef_grad
```

```python
import jax
import jax.numpy as jnp
from jax import lax
from jax.experimental import pallas as pl
from jax.experimental.pallas import tpu as pltpu
from jax.sharding import PartitionSpec as P

MESH = pl.DeviceIdType.MESH
NZ = 16
NY = 4
NC = 8
ROWS = 8
CH = NZ * ROWS
U = 512
W = 1024
L = 128


def near_first(i):
    k = i // 2 + 1
    odd = lax.rem(i, 2)
    return k * (1 - odd) + (NZ - k) * odd


def kernel(
    coef_ref, mant_ref, exp_ref, lin_ref, quad_ref, cross_ref, ply_ref, cot_ref,
    grad_ref, cgrad_ref,
    cases, fields, stress, weight, dst, own, part, pull, zsum, zpart, zpull, facs, cpart,
    ystat, mstat, zstat,
    load_sem, home_sem, ag_s, ag_r, fw_s, fw_r, ys_s, ys_r, zs_s, zs_r, py_s, py_r, pz_s, pz_r, cg_s, cg_r,
):
    case = lax.axis_index("case")
    elem = lax.axis_index("elem")
    y = elem // NZ
    z = lax.rem(elem, NZ)

    def z_peer(d):
        return (case, y * NZ + lax.rem(z + d, NZ))

    def y_peer(d):
        return (case, lax.rem(y + d, NY) * NZ + z)

    def c_peer(d):
        return (lax.rem(case + d, NC), elem)

    def remote(src, dst_, s, r, dev):
        return pltpu.make_async_remote_copy(
            src_ref=src, dst_ref=dst_, send_sem=s, recv_sem=r, device_id=dev, device_id_type=MESH
        )

    load = pltpu.make_async_copy(mant_ref, fields, load_sem)
    load.start()

    barrier = pltpu.get_barrier_semaphore()

    def greet(n, peer):
        def body(d, c):
            pl.semaphore_signal(barrier, inc=1, device_id=peer(d), device_id_type=MESH)
            return c

        lax.fori_loop(1, n, body, 0)

    greet(NZ, z_peer)
    greet(NY, y_peer)
    greet(NC, c_peer)
    pl.semaphore_wait(barrier, NZ + NY + NC - 3)

    def rows_of(yy, zz):
        return pl.ds(pl.multiple_of((yy * NZ + zz) * ROWS, ROWS), ROWS)

    def chunk_of(yy):
        return pl.ds(pl.multiple_of(yy * CH, CH), CH)

    def ag_copy(d):
        return remote(coef_ref, cases.at[rows_of(y, z)], ag_s.at[d], ag_r.at[d], z_peer(d))

    def ag_send(i, c):
        ag_copy(near_first(NZ - 2 - i)).start()
        return c

    lax.fori_loop(0, NZ - 1, ag_send, 0)
    home = pltpu.make_async_copy(coef_ref, cases.at[rows_of(y, z)], home_sem)
    home.start()

    def forward(src, zz):
        for d in (2, 1, 3):
            remote(src, cases.at[rows_of(y, zz)], fw_s.at[d], fw_r.at[d], y_peer(d)).start()

    forward(coef_ref, z)

    load.wait()
    eye = lax.broadcasted_iota(jnp.int32, (L, L), 0) == lax.broadcasted_iota(jnp.int32, (L, L), 1)

    def column(row):
        return jnp.sum(jnp.where(eye, jnp.broadcast_to(row, (L, L)), 0.0), axis=1, keepdims=True)

    def as_row(col):
        return jnp.sum(jnp.where(eye, jnp.broadcast_to(col, (L, L)), 0.0), axis=0, keepdims=True)

    for k in range(3):
        def scale(b, c, k=k):
            lanes = pl.ds(pl.multiple_of(b * L, L), L)
            gains = jnp.exp2(exp_ref[k, pl.ds(b, 1), :].astype(jnp.float32))
            for r in range(U // L):
                gain = column(gains[:, r * L : (r + 1) * L])
                block = fields[k, r * L : (r + 1) * L, lanes].astype(jnp.float32)
                fields[k, r * L : (r + 1) * L, lanes] = (block * gain).astype(jnp.bfloat16)
            return c

        lax.fori_loop(0, W // L, scale, 0)

    home.wait()

    def ag_take(i, c):
        d = near_first(i)
        zz = lax.rem(z + NZ - d, NZ)
        remote(coef_ref, cases.at[rows_of(y, zz)], ag_s.at[d], ag_r.at[d], z_peer(d)).wait_recv()
        forward(cases.at[rows_of(y, zz)], zz)
        return c

    lax.fori_loop(0, NZ - 1, ag_take, 0)

    def chunk(q, c):
        dy = q + (q // 2) * (5 - 2 * q)
        src = lax.rem(y + NY - dy, NY)
        rows = chunk_of(src)
        back = lax.rem(NY - dy, NY)

        @pl.when(q > 0)
        def _():
            remote(cases.at[rows], cases.at[rows], fw_s.at[dy], fw_r.at[dy], y_peer(dy)).wait_recv()

        a = cases[rows, :]
        for k in range(3):
            stress[k, rows, :] = jnp.dot(a, fields[k], preferred_element_type=jnp.float32)

        def index_of(j, top):
            lanes = pl.ds(pl.multiple_of(j * L, L), L)
            s1 = stress[0, rows, lanes]
            s2 = stress[1, rows, lanes]
            t = stress[2, rows, lanes]
            one = lin_ref[0:1, lanes] + quad_ref[0:1, lanes] * s1 + (2.0 * cross_ref[0:1, lanes]) * s2
            two = lin_ref[1:2, lanes] + quad_ref[1:2, lanes] * s2
            index = s1 * one + s2 * two + quad_ref[2:3, lanes] * (t * t)
            weight[rows, lanes] = index
            return jnp.maximum(top, index)

        top = lax.fori_loop(0, W // L, index_of, jnp.full((CH, L), -jnp.inf, jnp.float32))
        peak = jnp.max(top, axis=1, keepdims=True)

        def weigh(j, total):
            lanes = pl.ds(pl.multiple_of(j * L, L), L)
            s1 = stress[0, rows, lanes]
            s2 = stress[1, rows, lanes]
            t = stress[2, rows, lanes]
            plies = (ply_ref[0:1, lanes] + 1).astype(jnp.float32)
            w = plies * jnp.exp(weight[rows, lanes] - peak)
            weight[rows, lanes] = w
            f12 = 2.0 * cross_ref[0:1, lanes]
            dst[0, :, lanes] = (
                w * (lin_ref[0:1, lanes] + (2.0 * quad_ref[0:1, lanes]) * s1 + f12 * s2)
            ).astype(jnp.bfloat16)
            dst[1, :, lanes] = (
                w * (lin_ref[1:2, lanes] + (2.0 * quad_ref[1:2, lanes]) * s2 + f12 * s1)
            ).astype(jnp.bfloat16)
            dst[2, :, lanes] = (w * ((2.0 * quad_ref[2:3, lanes]) * t)).astype(jnp.bfloat16)
            return total + w

        total = lax.fori_loop(0, W // L, weigh, jnp.zeros((CH, L), jnp.float32))
        total = jnp.sum(total, axis=1, keepdims=True)
        ystat[0, pl.ds(src, 1), :] = as_row(peak)
        ystat[0, pl.ds(NY + src, 1), :] = as_row(total)

        @pl.when(q == NY - 1)
        def _():
            for d in (2, 1, 3):
                remote(ystat.at[0], ystat.at[d], ys_s.at[d], ys_r.at[d], y_peer(d)).start()

        terms = sum(
            lax.dot_general(
                dst[k], fields[k], (((1,), (1,)), ((), ())), preferred_element_type=jnp.float32
            )
            for k in range(3)
        )

        @pl.when(q == 0)
        def _():
            own[...] = terms

        @pl.when(q > 0)
        def _():
            part[back] = terms.astype(jnp.bfloat16)
            remote(part.at[back], pull.at[back], py_s.at[back], py_r.at[back], y_peer(back)).start()

        return c

    lax.fori_loop(0, NY, chunk, 0)

    for d in (1, 3, 2):
        remote(ystat.at[0], ystat.at[d], ys_s.at[d], ys_r.at[d], y_peer(d)).wait_recv()
    mid = jnp.max(ystat[:, 0:NY, :], axis=0)
    mstat[0:NY, :] = mid
    mstat[NY:, :] = jnp.sum(ystat[:, NY:, :] * jnp.exp(ystat[:, 0:NY, :] - mid[None]), axis=0)
    zstat[0] = mstat[...]

    def zs_copy(d):
        return remote(mstat, zstat.at[d], zs_s.at[d], zs_r.at[d], z_peer(d))

    def zs_send(i, c):
        zs_copy(near_first(NZ - 2 - i)).start()
        return c

    lax.fori_loop(0, NZ - 1, zs_send, 0)

    mid_y = mstat[pl.ds(y, 1), :]

    def share(d):
        return column(jnp.exp(ystat[d, pl.ds(y, 1), :] - mid_y))

    merged = own[...] * share(0)
    for d in (1, 3, 2):
        remote(part.at[d], pull.at[d], py_s.at[d], py_r.at[d], y_peer(d)).wait_recv()
        merged = merged + pull[d].astype(jnp.float32) * share(d)
    merged = merged.reshape(NZ, ROWS, U)
    zsum[...] = merged
    zpart[...] = merged.astype(jnp.bfloat16)

    def pz_copy(d):
        return remote(
            zpart.at[lax.rem(z + d, NZ)], zpull.at[d], pz_s.at[d], pz_r.at[d], z_peer(d)
        )

    def pz_send(i, c):
        pz_copy(near_first(NZ - 2 - i)).start()
        return c

    lax.fori_loop(0, NZ - 1, pz_send, 0)

    def zs_take(d, c):
        zs_copy(d).wait_recv()
        return c

    lax.fori_loop(1, NZ, zs_take, 0)
    peak = jnp.max(zstat[:, 0:NY, :], axis=0)
    total = jnp.sum(zstat[:, NY:, :] * jnp.exp(zstat[:, 0:NY, :] - peak[None]), axis=0)
    cot = cot_ref[...] / total
    factor = cot * jnp.exp(ystat[0, 0:NY, :] - peak)
    for r in range(NY):
        facs[r * L : (r + 1) * L, :] = jnp.broadcast_to(column(factor[r : r + 1, :]), (L, L))

    def coefs(j, c):
        lanes = pl.ds(pl.multiple_of(j * L, L), L)
        acc = [jnp.zeros((8, L), jnp.float32) for _ in range(6)]
        for r in range(NY):
            rows = slice(r * L, (r + 1) * L)
            w = weight[rows, lanes] * facs[rows, :]
            s1 = stress[0, rows, lanes]
            s2 = stress[1, rows, lanes]
            t = stress[2, rows, lanes]
            w1 = w * s1
            w2 = w * s2
            for n, v in enumerate((w1, w2, w1 * s1, w2 * s2, w * t * t, w1 * (2.0 * s2))):
                acc[n] = acc[n] + jnp.sum(v.reshape(L // 8, 8, L), axis=0)
        for n in range(6):
            cpart[case, n : n + 1, lanes] = jnp.sum(acc[n], axis=0, keepdims=True)
        return c

    lax.fori_loop(0, W // L, coefs, 0)

    def cg_copy(d):
        return remote(cpart.at[case], cpart.at[case], cg_s.at[d], cg_r.at[d], c_peer(d))

    for d in (4, 3, 5, 2, 6, 1, 7):
        cg_copy(d).start()

    pick = lax.broadcasted_iota(jnp.int32, (ROWS, L), 1) == z * ROWS + lax.broadcasted_iota(
        jnp.int32, (ROWS, L), 0
    )
    gain_y = jnp.sum(jnp.where(lax.broadcasted_iota(jnp.int32, (NY, L), 0) == y, cot, 0.0), axis=0, keepdims=True)
    peak_y = jnp.sum(jnp.where(lax.broadcasted_iota(jnp.int32, (NY, L), 0) == y, peak, 0.0), axis=0, keepdims=True)

    def gain(d):
        row = gain_y * jnp.exp(zstat[d, pl.ds(y, 1), :] - peak_y)
        return jnp.sum(jnp.where(pick, jnp.broadcast_to(row, (ROWS, L)), 0.0), axis=1, keepdims=True)

    def pz_take(i, acc):
        d = near_first(i)
        pz_copy(d).wait_recv()
        return acc + zpull[d].astype(jnp.float32) * gain(d)

    grad_ref[...] = lax.fori_loop(0, NZ - 1, pz_take, zsum[z] * gain(0))

    for d in range(1, NC):
        src = lax.rem(case + NC - d, NC)
        remote(cpart.at[src], cpart.at[src], cg_s.at[d], cg_r.at[d], c_peer(d)).wait_recv()
    cgrad_ref[...] = jnp.sum(cpart[...], axis=0)

    def sent(d, c):
        ag_copy(d).wait_send()
        zs_copy(d).wait_send()
        pz_copy(d).wait_send()
        return c

    lax.fori_loop(1, NZ, sent, 0)
    rows = chunk_of(y)
    for d in range(1, NY):
        remote(cases.at[rows], cases.at[rows], fw_s.at[d], fw_r.at[d], y_peer(d)).wait_send()
        remote(ystat.at[0], ystat.at[d], ys_s.at[d], ys_r.at[d], y_peer(d)).wait_send()
        remote(part.at[d], pull.at[d], py_s.at[d], py_r.at[d], y_peer(d)).wait_send()
    for d in range(1, NC):
        cg_copy(d).wait_send()


def per_device(load_coef, mantissa, scale_exp, lin_coef, quad_coef, cross_coef, ply_count, cotangent):
    f32, bf16 = jnp.float32, jnp.bfloat16
    vmem = pl.BlockSpec(memory_space=pltpu.VMEM)
    dma = pltpu.SemaphoreType.DMA
    return pl.pallas_call(
        kernel,
        out_shape=(
            jax.ShapeDtypeStruct((ROWS, U), f32),
            jax.ShapeDtypeStruct((6, W), f32),
        ),
        in_specs=[vmem, pl.BlockSpec(memory_space=pl.ANY)] + [vmem] * 6,
        out_specs=(vmem, vmem),
        scratch_shapes=[
            pltpu.VMEM((NY * CH, U), bf16),
            pltpu.VMEM((3, U, W), bf16),
            pltpu.VMEM((3, NY * CH, W), f32),
            pltpu.VMEM((NY * CH, W), f32),
            pltpu.VMEM((3, CH, W), bf16),
            pltpu.VMEM((CH, U), f32),
            pltpu.VMEM((NY, CH, U), bf16),
            pltpu.VMEM((NY, CH, U), bf16),
            pltpu.VMEM((NZ, ROWS, U), f32),
            pltpu.VMEM((NZ, ROWS, U), bf16),
            pltpu.VMEM((NZ, ROWS, U), bf16),
            pltpu.VMEM((NY * CH, L), f32),
            pltpu.VMEM((NC, 6, W), f32),
            pltpu.VMEM((NY, 2 * NY, L), f32),
            pltpu.VMEM((2 * NY, L), f32),
            pltpu.VMEM((NZ, 2 * NY, L), f32),
            dma, dma, dma((NZ,)), dma((NZ,)), dma((NY,)), dma((NY,)), dma((NY,)), dma((NY,)),
            dma((NZ,)), dma((NZ,)), dma((NY,)), dma((NY,)), dma((NZ,)), dma((NZ,)), dma((NC,)), dma((NC,)),
        ],
        compiler_params=pltpu.CompilerParams(
            collective_id=0, has_side_effects=True, vmem_limit_bytes=56 << 20
        ),
        name="envelope_grad",
    )(
        load_coef,
        jnp.transpose(mantissa, (1, 0, 2)),
        jnp.transpose(scale_exp, (1, 2, 0)),
        lin_coef,
        quad_coef,
        cross_coef.reshape(1, -1),
        ply_count.reshape(1, -1),
        cotangent.reshape(NY, L),
    )


def solution(mesh):
    return jax.shard_map(
        per_device,
        mesh=mesh,
        in_specs=(
            P(("case", "elem"), None),
            P(None, None, "elem"),
            P(None, None, "elem"),
            P(None, "elem"),
            P(None, "elem"),
            P("elem"),
            P("elem"),
            P("case"),
        ),
        out_specs=(P(("case", "elem"), None), P(None, "elem")),
        check_vma=False,
    )
```
